32 devices in a mesh: dp: 4 (over y, core), fsdp: 4 (over z), tensor: 2 (over x).
Axes of the slice: x: 2, y: 2, z: 4, core: 2. Of those that a mesh axis runs over, the one named last changes fastest.
Arguments:
- hidden_in: bfloat16 [7168, 8192], P(('dp', 'fsdp')), may hold values from -6 to 6
- queries: bfloat16 [7168, 8192], P(('dp', 'fsdp'), 'tensor')
- keys: bfloat16 [7168, 1024], P(('dp', 'fsdp'), 'tensor')
- output_gradient: bfloat16 [7168, 8192], P(('dp', 'fsdp'), 'tensor'), may hold values from -6 to 6
- rewards: float32 [16], P(('dp', 'fsdp')), may hold values from 0 to 4
- lengths: int32 [16], P(('dp', 'fsdp')), may hold values from 112 to 448
- master: float32 [8192, 1024], P(('dp', 'fsdp'), 'tensor'), may hold values from -0.0625 to 0.0625
- moment: float32 [8192, 1024], P(('dp', 'fsdp'), 'tensor'), may hold values from -6 to 6
- adam_second_moment: float32 [8192, 1024], P(('dp', 'fsdp'), 'tensor'), may hold values from 0.25 to 4
- layout: int32 [8], replicated, may hold values from 0 to 7, each once
Outputs:
- updated_master_weight: float32 [8192, 1024], P(('dp', 'fsdp'), 'tensor')
- new_moment: float32 [8192, 1024], P(('dp', 'fsdp'), 'tensor')
- new_second: float32 [8192, 1024], P(('dp', 'fsdp'), 'tensor')
- rollout_value_weight: bfloat16 [8192, 1024], P(('dp', 'fsdp'), 'tensor')
The draws below stay inside these ranges and needn't reach their ends.
All inputs are finite; a program needn't handle non-finite values.
Results may differ from the reference program's by a relative error of at most 0.0014.
Values may be sent and summed in bfloat16 or wider, within the bound.
A program may use at most 192 MiB of HBM per device.

```python
import math
import jax
import jax.numpy as jnp
from jax import lax

MODEL_WIDTH = 8192
QUERY_HEADS = 64
KEY_VALUE_HEADS = 8
HEAD_SIZE = 128
SEQUENCE_TOKENS = 448
QUERY_PER_VALUE = 8
BATCH_SEQUENCES = 16
TOKEN_SLOTS = 7168


def query_key_pair(key):
    key_portion = jax.random.normal(jax.random.fold_in(key, 11), (BATCH_SEQUENCES, SEQUENCE_TOKENS, KEY_VALUE_HEADS, HEAD_SIZE), jnp.float32)
    query_portion = jax.random.normal(jax.random.fold_in(key, 12), (BATCH_SEQUENCES, SEQUENCE_TOKENS, KEY_VALUE_HEADS, QUERY_PER_VALUE, HEAD_SIZE), jnp.float32)
    return (query_portion, key_portion)


def draw_queries(key, part):
    query_portion, key_portion = query_key_pair(key)
    return query_portion.reshape(TOKEN_SLOTS, QUERY_HEADS * HEAD_SIZE).astype(jnp.bfloat16)


def draw_keys(key, part):
    query_portion, key_portion = query_key_pair(key)
    return key_portion.reshape(TOKEN_SLOTS, KEY_VALUE_HEADS * HEAD_SIZE).astype(jnp.bfloat16)


def plant(result, stream_key, smallest, high):
    extent = result.shape
    spot = [jax.random.randint(jax.random.fold_in(stream_key, axis), (), 0, extent[axis]) for axis in range(len(extent))]
    result = result.at[tuple(spot)].set(smallest)
    longest = extent.index(max(extent))
    spot[longest] = (spot[longest] + 1) % extent[longest]
    return result.at[tuple(spot)].set(high)


def steps_of(key, extent, shards, smallest, top_value):
    def one(dim, shards_of):
        steps = jax.random.uniform(jax.random.fold_in(jax.random.fold_in(key, 6), dim), (shards_of,), jnp.float32, smallest / len(shards), top_value / len(shards))
        return jnp.repeat(jnp.exp(steps), extent[dim] // shards_of).reshape((-1,) + (1,) * (len(extent) - dim - 1))

    factor_of = one(*shards[0])
    for cut in shards[1:]:
        factor_of = factor_of * one(*cut)
    return factor_of


def scatter_about(key, shape, spread, limit, split=(), held_as=jnp.bfloat16):
    gain = steps_of(key, shape, split, -0.22, 0.18) if split else 1.0
    array = jax.random.normal(key, shape, jnp.float32) * spread * gain
    return jnp.minimum(jnp.maximum(array, -limit), limit).astype(held_as)


def setup_inputs(seed: int = 0) -> dict:
    splits = jax.random.split(jax.random.key(seed), 11)
    hidden_in = scatter_about(splits[0], (TOKEN_SLOTS, MODEL_WIDTH), 1.0, 6.0, ((0, 16),))
    queries = draw_queries(jax.random.fold_in(splits[10], 71), 0)
    keys = draw_keys(jax.random.fold_in(splits[10], 71), 0)
    output_gradient = scatter_about(splits[3], (TOKEN_SLOTS, QUERY_HEADS * HEAD_SIZE), 1.0, 6.0, ((0, 16), (1, 2)))
    rewards = jnp.clip(4.0 * jax.random.uniform(splits[4], (BATCH_SEQUENCES,), jnp.float32) ** steps_of(splits[4], (BATCH_SEQUENCES,), ((0, 16),), -0.2, 0.2), 0.0, 4.0)
    lengths = plant(jax.random.randint(splits[5], (BATCH_SEQUENCES,), max(6, SEQUENCE_TOKENS // 4), SEQUENCE_TOKENS + 1), jax.random.fold_in(splits[5], 1), max(6, SEQUENCE_TOKENS // 4), SEQUENCE_TOKENS).astype(jnp.int32)
    master = scatter_about(splits[6], (MODEL_WIDTH, KEY_VALUE_HEADS * HEAD_SIZE), MODEL_WIDTH ** -0.5, 0.0625, ((0, 16), (1, 2)), jnp.float32)
    moment = scatter_about(splits[7], (MODEL_WIDTH, KEY_VALUE_HEADS * HEAD_SIZE), 1.0, 6.0, ((0, 16), (1, 2)), jnp.float32)
    adam_second_moment = jnp.clip(jnp.exp(math.log(4.0) - 2.7725887 * jax.random.uniform(splits[8], (MODEL_WIDTH, KEY_VALUE_HEADS * HEAD_SIZE), jnp.float32) ** steps_of(splits[8], (MODEL_WIDTH, KEY_VALUE_HEADS * HEAD_SIZE), ((0, 16), (1, 2)), -0.2, 0.2)), 0.25, 4.0)
    layout = jax.random.permutation(splits[9], KEY_VALUE_HEADS).astype(jnp.int32)
    return dict(hidden_in=hidden_in, queries=queries, keys=keys, output_gradient=output_gradient, rewards=rewards, lengths=lengths, master=master, moment=moment, adam_second_moment=adam_second_moment, layout=layout)


def sequence_value_grad(query_matrix, key_matrix, out_rows, value_weight, length):
    token_slot_index = query_matrix.shape[0]
    query_head_rows = query_matrix.reshape(token_slot_index, KEY_VALUE_HEADS, QUERY_PER_VALUE, HEAD_SIZE).astype(jnp.float32)
    key_head_rows = key_matrix.reshape(token_slot_index, KEY_VALUE_HEADS, HEAD_SIZE).astype(jnp.float32)
    scores = jnp.einsum('tkgd,skd->kgts', query_head_rows, key_head_rows) / jnp.sqrt(jnp.float32(HEAD_SIZE))
    position = jnp.arange(token_slot_index)
    allowed = (position[None, :] <= position[:, None]) & (position[None, :] < length)
    scores = jnp.where(allowed[None, None], scores, jnp.float32(-1e+30))
    top = lax.optimization_barrier(jnp.max(scores, axis=-1, keepdims=True))
    expo = jnp.exp(scores - top)
    probs = (expo / lax.optimization_barrier(jnp.sum(expo, axis=-1, keepdims=True))).astype(jnp.bfloat16)
    attention_gradient = (value_weight[:, None] * out_rows.astype(jnp.float32)).astype(jnp.bfloat16)
    head_gradient = attention_gradient.reshape(token_slot_index, KEY_VALUE_HEADS, QUERY_PER_VALUE, HEAD_SIZE).astype(jnp.float32)
    value_gradient = jnp.einsum('kgts,tkgd->skd', probs.astype(jnp.float32), head_gradient)
    return value_gradient.reshape(token_slot_index, KEY_VALUE_HEADS * HEAD_SIZE).astype(jnp.bfloat16)

def reference(hidden_in, queries, keys, output_gradient, rewards, lengths, master, moment, adam_second_moment, layout):
    mean_reward = jnp.sum(rewards) / BATCH_SEQUENCES
    total = jnp.sum(lengths).astype(jnp.float32)
    advantage = rewards - mean_reward
    position = jnp.arange(SEQUENCE_TOKENS)
    valid = position[None, :] < lengths[:, None]
    value_weight = jnp.where(valid, advantage[:, None] * BATCH_SEQUENCES / total, jnp.float32(0.0))

    def unit_value(items):
        query_matrix, key_matrix, out_rows, row_weight, length = items
        return sequence_value_grad(query_matrix, key_matrix, out_rows, row_weight, length)
    value_gradient = lax.map(unit_value, (queries.reshape(BATCH_SEQUENCES, SEQUENCE_TOKENS, QUERY_HEADS * HEAD_SIZE), keys.reshape(BATCH_SEQUENCES, SEQUENCE_TOKENS, KEY_VALUE_HEADS * HEAD_SIZE), output_gradient.reshape(BATCH_SEQUENCES, SEQUENCE_TOKENS, QUERY_HEADS * HEAD_SIZE), value_weight, lengths))
    value_gradient = value_gradient.reshape(TOKEN_SLOTS, KEY_VALUE_HEADS * HEAD_SIZE)
    grad = lax.dot_general(hidden_in, value_gradient, (((0,), (0,)), ((), ())), preferred_element_type=jnp.float32)
    new_moment = 0.9 * moment + 0.1 * grad
    new_second = 0.95 * adam_second_moment + 0.05 * grad * grad
    corrected = new_moment / (1.0 - 0.9 ** 10) / (jnp.sqrt(new_second / (1.0 - 0.95 ** 10)) + 1e-08)
    updated_master_weight = master - 0.002 * (corrected + 0.1 * master)
    rounded_weight = updated_master_weight.astype(jnp.bfloat16).reshape(MODEL_WIDTH, KEY_VALUE_HEADS, HEAD_SIZE)
    rollout_value_weight = rounded_weight[:, layout, :].reshape(MODEL_WIDTH, KEY_VALUE_HEADS * HEAD_SIZE)
    return (updated_master_weight, new_moment, new_second, rollout_value_weight)
```

```python
import functools
import math

import jax
import jax.numpy as jnp
from jax import lax
from jax.experimental import pallas as pl
from jax.experimental.pallas import tpu as pltpu
from jax.sharding import PartitionSpec as P

HEAD_SIZE = 128
QUERY_PER_VALUE = 8
AXES = ("dp", "fsdp")
MESH = pl.DeviceIdType.MESH
F32 = jnp.float32
BF16 = jnp.bfloat16


def log2_of(number):
    return number.bit_length() - 1


def adam(grad, moment, second, master):
    new_moment = 0.9 * moment + 0.1 * grad
    new_second = 0.95 * second + 0.05 * grad * grad
    corrected = new_moment / (1.0 - 0.9**10) / (jnp.sqrt(new_second / (1.0 - 0.95**10)) + 1e-08)
    return new_moment, new_second, master - 0.002 * (corrected + 0.1 * master)


def query_blocks(slots):
    blocks = []
    for start in range(0, slots, 256):
        size = min(256, slots - start)
        blocks.append((start, size, start + size))
    return blocks


def step_kernel(
    sizes,
    rewards_ref,
    lengths_ref,
    layout_ref,
    hidden_hbm,
    queries_hbm,
    keys_ref,
    outgrad_hbm,
    master_ref,
    moment_ref,
    second_ref,
    weight_out,
    moment_out,
    second_out,
    rollout_out,
    hidden,
    queries,
    outgrad,
    bias,
    value_acc,
    value_t,
    part,
    landed,
    heads_all,
    scalar_sent,
    scalar_landed,
    load_sem,
    rs_send,
    rs_recv,
    scalar_send,
    scalar_recv,
    swap_send,
    swap_recv,
):
    dp_count, fsdp_count, tensor_count = sizes
    dp, fsdp, tensor = (lax.axis_index(a) for a in ("dp", "fsdp", "tensor"))
    dp_bits, fsdp_bits = log2_of(dp_count), log2_of(fsdp_count)
    stages = dp_bits + fsdp_bits
    blocks = dp_count * fsdp_count
    slots = hidden_hbm.shape[0]
    rows = master_ref.shape[0]
    heads = keys_ref.shape[1] // HEAD_SIZE
    group = QUERY_PER_VALUE * HEAD_SIZE

    bits, partners = [], []
    for k in range(stages):
        name, index, shift = ("dp", dp, k) if k < dp_bits else ("fsdp", fsdp, k - dp_bits)
        bit = (index // (1 << shift)) % 2
        bits.append(bit)
        partners.append({name: index + (1 - 2 * bit) * (1 << shift)})
    peers = [{"tensor": (tensor + d) % tensor_count} for d in range(1, tensor_count)]

    loads = []
    for c in range(heads):
        columns = pl.ds(c * group, group)
        loads.append(
            [
                pltpu.make_async_copy(source.at[:, columns], target.at[:, columns], load_sem.at[2 * c + i])
                for i, (source, target) in enumerate(((queries_hbm, queries), (outgrad_hbm, outgrad)))
            ]
        )
    hidden_load = pltpu.make_async_copy(hidden_hbm, hidden, load_sem.at[2 * heads])
    for copy in loads[0]:
        copy.start()
    hidden_load.start()
    for pair in loads[1:]:
        for copy in pair:
            copy.start()

    barrier = pltpu.get_barrier_semaphore()
    for target in partners + peers:
        pl.semaphore_signal(barrier, inc=1, device_id=target, device_id_type=MESH)

    length = lengths_ref[0]
    own_reward = jnp.full((8, 128), rewards_ref[0], F32)
    own_length = jnp.full((8, 128), length, jnp.int32).astype(F32)
    tile_row = lax.broadcasted_iota(jnp.int32, (8, 128), 0)
    totals = jnp.where(tile_row == 0, own_reward, own_length)

    key_pos = lax.broadcasted_iota(jnp.int32, (slots, slots), 0)
    query_pos = lax.broadcasted_iota(jnp.int32, (slots, slots), 1)
    bias[...] = jnp.where((key_pos <= query_pos) & (key_pos < length), 0.0, -1e30).astype(F32)
    exponent = F32(math.log2(math.e) / math.sqrt(HEAD_SIZE))

    pl.semaphore_wait(barrier, stages + tensor_count - 1)

    def scalar_copy(k):
        return pltpu.make_async_remote_copy(
            src_ref=scalar_sent.at[k],
            dst_ref=scalar_landed.at[k],
            send_sem=scalar_send.at[k],
            recv_sem=scalar_recv.at[k],
            device_id=partners[k],
            device_id_type=MESH,
        )

    def query_head(c, j):
        offset = pl.multiple_of((c * QUERY_PER_VALUE + j) * HEAD_SIZE, HEAD_SIZE)
        columns = pl.ds(offset, HEAD_SIZE)
        for start, size, seen in query_blocks(slots):
            scores = lax.dot_general(
                keys_ref[:seen, c * HEAD_SIZE : (c + 1) * HEAD_SIZE],
                queries[start : start + size, columns],
                (((1,), (1,)), ((), ())),
                preferred_element_type=F32,
            )
            scores = scores + bias[:seen, start : start + size]
            top = jnp.max(scores, axis=0, keepdims=True)
            expo = jnp.exp2((scores - top) * exponent)
            total = jnp.sum(expo, axis=0, keepdims=True)
            slot = start + lax.broadcasted_iota(jnp.int32, (1, size), 1)
            inverse = jnp.where(slot < length, 1.0 / total, 0.0)
            probs = (expo * inverse).astype(BF16)
            value_acc[:seen, :] += jnp.dot(
                probs, outgrad[start : start + size, columns], preferred_element_type=F32
            )

    def attention(c, first, last):
        @pl.loop(first, last)
        def _(j):
            query_head(c, j)

    def rows_of(position):
        bit = [(position // (1 << (stages - 1 - k))) % 2 for k in range(stages)]
        dp_of = sum(bit[k] * (1 << k) for k in range(dp_bits))
        fsdp_of = sum(bit[dp_bits + k] * (1 << k) for k in range(fsdp_bits))
        return dp_of * fsdp_count + fsdp_of

    sent_at, kept_at, land_at, half_of = [], [], [], []
    base, landing = 0, 0
    for k in range(stages):
        half = blocks >> (k + 1)
        sent_at.append(base + (1 - bits[k]) * half)
        base = base + bits[k] * half
        kept_at.append(base)
        half_of.append(half)
        land_at.append(landing)
        landing += half

    def reduce_copy(k, c):
        return pltpu.make_async_remote_copy(
            src_ref=part.at[c, pl.ds(sent_at[k], half_of[k])],
            dst_ref=landed.at[c, pl.ds(land_at[k], half_of[k])],
            send_sem=rs_send.at[k, c],
            recv_sem=rs_recv.at[k, c],
            device_id=partners[k],
            device_id_type=MESH,
        )

    def multiply(c, begin, count):
        @pl.loop(0, count)
        def _(i):
            position = begin + i
            columns = pl.ds(pl.multiple_of(rows_of(position) * rows, 128), rows)
            part[c, position] = jnp.dot(
                value_t[...], hidden[:, columns], preferred_element_type=F32
            ).astype(BF16)

    def fold(k, c, begin, count):
        @pl.loop(0, count)
        def _(i):
            position = begin + i
            arrived = landed[c, land_at[k] + position - kept_at[k]]
            part[c, position] = (part[c, position].astype(F32) + arrived.astype(F32)).astype(BF16)

    def advance(k, c):
        reduce_copy(k, c).wait_recv()
        fold(k, c, sent_at[k + 1], half_of[k + 1])
        reduce_copy(k + 1, c).start()
        fold(k, c, kept_at[k + 1], half_of[k + 1])

    def swap_copy(d, c):
        return pltpu.make_async_remote_copy(
            src_ref=heads_all.at[c],
            dst_ref=heads_all.at[d * heads + c],
            send_sem=swap_send.at[d - 1, c],
            recv_sem=swap_recv.at[d - 1, c],
            device_id=peers[d - 1],
            device_id_type=MESH,
        )

    def finish(c):
        k = stages - 1
        reduce_copy(k, c).wait_recv()
        total = part[c, kept_at[k]].astype(F32) + landed[c, land_at[k]].astype(F32)
        columns = slice(c * HEAD_SIZE, (c + 1) * HEAD_SIZE)
        new_moment, new_second, weight = adam(
            total.T, moment_ref[:, columns], second_ref[:, columns], master_ref[:, columns]
        )
        heads_all[c] = weight.astype(BF16)
        for d in range(1, tensor_count):
            swap_copy(d, c).start()
        moment_out[:, columns] = new_moment
        second_out[:, columns] = new_second
        weight_out[:, columns] = weight

    share = -(-QUERY_PER_VALUE // stages)
    for c in range(heads):
        for copy in loads[c]:
            copy.wait()
        value_acc[...] = jnp.zeros_like(value_acc)
        if c == 0:
            done = 0
            for k in range(stages):
                scalar_sent[k] = totals
                scalar_copy(k).start()
                last = min(QUERY_PER_VALUE, done + share)
                attention(c, done, last)
                done = last
                scalar_copy(k).wait_recv()
                totals = totals + scalar_landed[k]
            if done < QUERY_PER_VALUE:
                attention(c, done, QUERY_PER_VALUE)
            count = F32(blocks)
            advantage = own_reward[:1] - totals[0:1] / count
            value_weight = advantage * count / totals[1:2]
            hidden_load.wait()
        else:
            attention(c, 0, QUERY_PER_VALUE)
            advance(0, c - 1)
        value_t[...] = (value_acc[...] * value_weight).T.astype(BF16)
        multiply(c, sent_at[0], half_of[0])
        reduce_copy(0, c).start()
        multiply(c, kept_at[0], half_of[0])
    advance(0, heads - 1)
    for step in range(heads + stages - 2):
        for k in reversed(range(1, stages)):
            c = step - (k - 1)
            if 0 <= c < heads:
                if k < stages - 1:
                    advance(k, c)
                else:
                    finish(c)

    for c in range(heads):
        for d in range(1, tensor_count):
            swap_copy(d, c).wait_recv()
    for c in range(heads):
        wanted = layout_ref[tensor * heads + c]
        back = (tensor - wanted // heads + tensor_count) % tensor_count
        rollout_out[:, c * HEAD_SIZE : (c + 1) * HEAD_SIZE] = heads_all[back * heads + wanted % heads]
    for k in range(stages):
        scalar_copy(k).wait_send()
        for c in range(heads):
            reduce_copy(k, c).wait_send()
    for c in range(heads):
        for d in range(1, tensor_count):
            swap_copy(d, c).wait_send()


def fused_step(
    sizes, hidden_in, queries, keys, output_gradient, rewards, lengths, master, moment, second, layout
):
    dp_count, fsdp_count, tensor_count = sizes
    blocks = dp_count * fsdp_count
    stages = log2_of(blocks)
    slots = hidden_in.shape[0]
    rows = master.shape[0]
    heads = keys.shape[1] // HEAD_SIZE
    smem = pl.BlockSpec(memory_space=pltpu.SMEM)
    vmem = pl.BlockSpec(memory_space=pltpu.VMEM)
    anywhere = pl.BlockSpec(memory_space=pl.ANY)
    dma = pltpu.SemaphoreType.DMA
    return pl.pallas_call(
        functools.partial(step_kernel, sizes),
        out_shape=[jax.ShapeDtypeStruct(master.shape, F32)] * 3
        + [jax.ShapeDtypeStruct(master.shape, BF16)],
        in_specs=[smem, smem, smem, anywhere, anywhere, vmem, anywhere, vmem, vmem, vmem],
        out_specs=[vmem] * 4,
        scratch_shapes=[
            pltpu.VMEM(hidden_in.shape, BF16),
            pltpu.VMEM(queries.shape, BF16),
            pltpu.VMEM(queries.shape, BF16),
            pltpu.VMEM((slots, slots), F32),
            pltpu.VMEM((slots, HEAD_SIZE), F32),
            pltpu.VMEM((HEAD_SIZE, slots), BF16),
            pltpu.VMEM((heads, blocks, HEAD_SIZE, rows), BF16),
            pltpu.VMEM((heads, blocks - 1, HEAD_SIZE, rows), BF16),
            pltpu.VMEM((tensor_count * heads, rows, HEAD_SIZE), BF16),
            pltpu.VMEM((stages, 8, 128), F32),
            pltpu.VMEM((stages, 8, 128), F32),
            dma((2 * heads + 1,)),
            dma((stages, heads)),
            dma((stages, heads)),
            dma((stages,)),
            dma((stages,)),
            dma((tensor_count - 1, heads)),
            dma((tensor_count - 1, heads)),
        ],
        compiler_params=pltpu.CompilerParams(
            collective_id=0, has_side_effects=True, vmem_limit_bytes=60 * 1024 * 1024
        ),
    )(rewards, lengths, layout, hidden_in, queries, keys, output_gradient, master, moment, second)


def value_grad(query_matrix, key_matrix, out_rows, value_weight, length):
    token_slot_index = query_matrix.shape[0]
    heads_local = key_matrix.shape[1] // HEAD_SIZE
    query_head_rows = query_matrix.reshape(
        token_slot_index, heads_local, QUERY_PER_VALUE, HEAD_SIZE
    )
    key_head_rows = key_matrix.reshape(token_slot_index, heads_local, HEAD_SIZE)
    scores = jnp.einsum(
        "tkgd,skd->kgts", query_head_rows, key_head_rows, preferred_element_type=jnp.float32
    ) / jnp.sqrt(jnp.float32(HEAD_SIZE))
    position = jnp.arange(token_slot_index)
    allowed = (position[None, :] <= position[:, None]) & (position[None, :] < length)
    scores = jnp.where(allowed[None, None], scores, jnp.float32(-1e30))
    top = jnp.max(scores, axis=-1, keepdims=True)
    expo = jnp.exp(scores - top)
    probs = (expo / jnp.sum(expo, axis=-1, keepdims=True)).astype(jnp.bfloat16)
    attention_gradient = (value_weight[:, None] * out_rows.astype(jnp.float32)).astype(jnp.bfloat16)
    head_gradient = attention_gradient.reshape(
        token_slot_index, heads_local, QUERY_PER_VALUE, HEAD_SIZE
    )
    value_gradient = jnp.einsum(
        "kgts,tkgd->skd", probs, head_gradient, preferred_element_type=jnp.float32
    )
    return value_gradient.reshape(token_slot_index, heads_local * HEAD_SIZE).astype(jnp.bfloat16)


def plain_step(
    hidden_in, queries, keys, output_gradient, rewards, lengths, master, moment, second, layout
):
    reward_sum, length_sum = lax.psum(
        (jnp.sum(rewards), jnp.sum(lengths).astype(jnp.float32)), AXES
    )
    seq_count = jnp.float32(lax.axis_size(AXES))
    advantage = rewards[0] - reward_sum / seq_count
    position = jnp.arange(hidden_in.shape[0])
    value_weight = jnp.where(
        position < lengths[0], advantage * seq_count / length_sum, jnp.float32(0.0)
    )
    value_gradient = value_grad(queries, keys, output_gradient, value_weight, lengths[0])
    grad = lax.psum_scatter(
        lax.dot_general(
            hidden_in, value_gradient, (((0,), (0,)), ((), ())), preferred_element_type=jnp.float32
        ),
        AXES,
        scatter_dimension=0,
        tiled=True,
    )
    new_moment, new_second, weight = adam(grad, moment, second, master)
    rounded = weight.astype(jnp.bfloat16)
    row_count = rounded.shape[0]
    heads_local = rounded.shape[1] // HEAD_SIZE
    targets = lax.dynamic_slice_in_dim(layout, lax.axis_index("tensor") * heads_local, heads_local)
    piece = lax.all_gather(rounded, "tensor", axis=1, tiled=True)
    piece_rows = piece.reshape(row_count, piece.shape[1] // HEAD_SIZE, HEAD_SIZE)
    rollout = jnp.take(piece_rows, targets, axis=1).reshape(row_count, heads_local * HEAD_SIZE)
    return weight, new_moment, new_second, rollout


def solution(mesh):
    sizes = tuple(mesh.shape[a] for a in ("dp", "fsdp", "tensor"))

    def on_device(hidden_in, *rest):
        rows = hidden_in.shape[1] // (sizes[0] * sizes[1])
        powers = all(size & (size - 1) == 0 for size in sizes[:2])
        if rows % 128 == 0 and powers and sizes[2] > 1:
            return tuple(fused_step(sizes, hidden_in, *rest))
        return plain_step(hidden_in, *rest)

    rows_spec, split_spec = P(AXES, None), P(AXES, "tensor")
    placed = (rows_spec,) + (split_spec,) * 3 + (P(AXES),) * 2 + (split_spec,) * 3 + (P(),)
    return jax.shard_map(
        on_device, mesh=mesh, in_specs=placed, out_specs=(split_spec,) * 4, check_vma=False
    )
```

```python
import functools
import math

import jax
import jax.numpy as jnp
from jax import lax
from jax.experimental import pallas as pl
from jax.experimental.pallas import tpu as pltpu
from jax.sharding import PartitionSpec as P

HEAD_SIZE = 128
QUERY_PER_VALUE = 8
AXES = ("dp", "fsdp")
MESH = pl.DeviceIdType.MESH
F32 = jnp.float32
BF16 = jnp.bfloat16


def log2_of(number):
    return number.bit_length() - 1


def adam(grad, moment, second, master):
    new_moment = 0.9 * moment + 0.1 * grad
    new_second = 0.95 * second + 0.05 * grad * grad
    corrected = new_moment / (1.0 - 0.9**10) / (jnp.sqrt(new_second / (1.0 - 0.95**10)) + 1e-08)
    return new_moment, new_second, master - 0.002 * (corrected + 0.1 * master)


def query_blocks(slots):
    blocks = []
    for start in range(0, slots, 256):
        size = min(256, slots - start)
        blocks.append((start, size, start + size))
    return blocks


def step_kernel(
    sizes,
    rewards_ref,
    lengths_ref,
    layout_ref,
    hidden_hbm,
    queries_hbm,
    keys_ref,
    outgrad_hbm,
    master_hbm,
    moment_hbm,
    second_hbm,
    grad_out,
    rollout_out,
    hidden,
    queries,
    outgrad,
    master_ref,
    moment_ref,
    second_ref,
    bias,
    value_acc,
    value_t,
    part,
    landed,
    heads_all,
    scalar_sent,
    scalar_landed,
    load_sem,
    rs_send,
    rs_recv,
    scalar_send,
    scalar_recv,
    swap_send,
    swap_recv,
):
    dp_count, fsdp_count, tensor_count = sizes
    dp, fsdp, tensor = (lax.axis_index(a) for a in ("dp", "fsdp", "tensor"))
    dp_bits, fsdp_bits = log2_of(dp_count), log2_of(fsdp_count)
    stages = dp_bits + fsdp_bits
    blocks = dp_count * fsdp_count
    slots = hidden_hbm.shape[0]
    rows = master_ref.shape[0]
    heads = keys_ref.shape[1] // HEAD_SIZE
    group = QUERY_PER_VALUE * HEAD_SIZE

    bits, partners = [], []
    for k in range(stages):
        name, index, shift = ("dp", dp, k) if k < dp_bits else ("fsdp", fsdp, k - dp_bits)
        bit = (index // (1 << shift)) % 2
        bits.append(bit)
        partners.append({name: index + (1 - 2 * bit) * (1 << shift)})
    others = [
        [{name: (index + d) % size} for d in range(1, size)]
        for name, index, size in (("dp", dp, dp_count), ("fsdp", fsdp, fsdp_count))
    ]
    peers = [{"tensor": (tensor + d) % tensor_count} for d in range(1, tensor_count)]

    loads = []
    for c in range(heads):
        columns = pl.ds(c * group, group)
        loads.append(
            [
                pltpu.make_async_copy(source.at[:, columns], target.at[:, columns], load_sem.at[2 * c + i])
                for i, (source, target) in enumerate(((queries_hbm, queries), (outgrad_hbm, outgrad)))
            ]
        )
    hidden_load = pltpu.make_async_copy(hidden_hbm, hidden, load_sem.at[2 * heads])
    for copy in loads[0]:
        copy.start()
    hidden_load.start()
    for pair in loads[1:]:
        for copy in pair:
            copy.start()
    state_loads = [
        pltpu.make_async_copy(source, target, load_sem.at[2 * heads + 1 + i])
        for i, (source, target) in enumerate(
            ((master_hbm, master_ref), (moment_hbm, moment_ref), (second_hbm, second_ref))
        )
    ]
    for copy in state_loads:
        copy.start()

    barrier = pltpu.get_barrier_semaphore()
    for target in others[0] + others[1] + peers:
        pl.semaphore_signal(barrier, inc=1, device_id=target, device_id_type=MESH)

    length = lengths_ref[0]
    own_reward = jnp.full((8, 128), rewards_ref[0], F32)
    own_length = jnp.full((8, 128), length, jnp.int32).astype(F32)
    tile_row = lax.broadcasted_iota(jnp.int32, (8, 128), 0)
    totals = jnp.where(tile_row == 0, own_reward, own_length)

    key_pos = lax.broadcasted_iota(jnp.int32, (slots, slots), 0)
    query_pos = lax.broadcasted_iota(jnp.int32, (slots, slots), 1)
    bias[...] = jnp.where((key_pos <= query_pos) & (key_pos < length), 0.0, -1e30).astype(F32)
    exponent = F32(math.log2(math.e) / math.sqrt(HEAD_SIZE))

    def scalar_copies(turn):
        first = turn * (dp_count - 1)
        return [
            pltpu.make_async_remote_copy(
                src_ref=scalar_sent.at[turn],
                dst_ref=scalar_landed.at[first + i],
                send_sem=scalar_send.at[first + i],
                recv_sem=scalar_recv.at[first + i],
                device_id=target,
                device_id_type=MESH,
            )
            for i, target in enumerate(others[turn])
        ]

    def send_scalars(turn, tile):
        scalar_sent[turn] = tile
        for copy in scalar_copies(turn):
            copy.start()

    def add_scalars(turn, tile):
        first = turn * (dp_count - 1)
        for i, copy in enumerate(scalar_copies(turn)):
            copy.wait_recv()
            tile = tile + scalar_landed[first + i]
        return tile

    def query_head(c, j):
        offset = pl.multiple_of((c * QUERY_PER_VALUE + j) * HEAD_SIZE, HEAD_SIZE)
        columns = pl.ds(offset, HEAD_SIZE)
        for start, size, seen in query_blocks(slots):
            scores = lax.dot_general(
                keys_ref[:seen, c * HEAD_SIZE : (c + 1) * HEAD_SIZE],
                queries[start : start + size, columns],
                (((1,), (1,)), ((), ())),
                preferred_element_type=F32,
            )
            scores = scores + bias[:seen, start : start + size]
            top = jnp.max(scores, axis=0, keepdims=True)
            expo = jnp.exp2((scores - top) * exponent)
            total = jnp.sum(expo, axis=0, keepdims=True)
            slot = start + lax.broadcasted_iota(jnp.int32, (1, size), 1)
            inverse = jnp.where(slot < length, 1.0 / total, 0.0)
            probs = (expo * inverse).astype(BF16)
            value_acc[c, :seen, :] += jnp.dot(
                probs, outgrad[start : start + size, columns], preferred_element_type=F32
            )

    def attention(c, first, last):
        @pl.loop(first, last, unroll=True)
        def _(j):
            query_head(c, j)

    def rows_of(position):
        bit = [(position // (1 << (stages - 1 - k))) % 2 for k in range(stages)]
        dp_of = sum(bit[k] * (1 << k) for k in range(dp_bits))
        fsdp_of = sum(bit[dp_bits + k] * (1 << k) for k in range(fsdp_bits))
        return dp_of * fsdp_count + fsdp_of

    sent_at, kept_at, land_at, half_of = [], [], [], []
    base, landing = 0, 0
    for k in range(stages):
        half = blocks >> (k + 1)
        sent_at.append(base + (1 - bits[k]) * half)
        base = base + bits[k] * half
        kept_at.append(base)
        half_of.append(half)
        land_at.append(landing)
        landing += half

    def reduce_copy(k, u):
        return pltpu.make_async_remote_copy(
            src_ref=part.at[u, pl.ds(sent_at[k], half_of[k])],
            dst_ref=landed.at[u, pl.ds(land_at[k], half_of[k])],
            send_sem=rs_send.at[k, u],
            recv_sem=rs_recv.at[k, u],
            device_id=partners[k],
            device_id_type=MESH,
        )

    def multiply(c, begin, count):
        @pl.loop(0, count)
        def _(i):
            position = begin + i
            columns = pl.ds(pl.multiple_of(rows_of(position) * rows, 128), rows)
            product = jnp.dot(
                value_t[...], hidden[:, columns], preferred_element_type=F32
            ).astype(BF16)
            part[2 * c, position] = product[: HEAD_SIZE // 2]
            part[2 * c + 1, position] = product[HEAD_SIZE // 2 :]

    def fold(k, u, begin, count):
        @pl.loop(0, count)
        def _(i):
            position = begin + i
            arrived = landed[u, land_at[k] + position - kept_at[k]]
            part[u, position] = (part[u, position].astype(F32) + arrived.astype(F32)).astype(BF16)

    def advance(k, u):
        reduce_copy(k, u).wait_recv()
        fold(k, u, sent_at[k + 1], half_of[k + 1])
        reduce_copy(k + 1, u).start()
        fold(k, u, kept_at[k + 1], half_of[k + 1])

    def swap_copy(d, c):
        return pltpu.make_async_remote_copy(
            src_ref=heads_all.at[c],
            dst_ref=heads_all.at[d * heads + c],
            send_sem=swap_send.at[d - 1, c],
            recv_sem=swap_recv.at[d - 1, c],
            device_id=peers[d - 1],
            device_id_type=MESH,
        )

    def arrive(u):
        k = stages - 1
        reduce_copy(k, u).wait_recv()
        return part[u, kept_at[k]].astype(F32) + landed[u, land_at[k]].astype(F32)

    def finish(c):
        total = jnp.concatenate([arrive(2 * c), arrive(2 * c + 1)], axis=0).T
        columns = slice(c * HEAD_SIZE, (c + 1) * HEAD_SIZE)
        _, _, weight = adam(
            total, moment_ref[:, columns], second_ref[:, columns], master_ref[:, columns]
        )
        heads_all[c] = weight.astype(BF16)
        for d in range(1, tensor_count):
            swap_copy(d, c).start()
        grad_out[:, columns] = total

    def attend(c, first=0, last=QUERY_PER_VALUE):
        if first == 0:
            for copy in loads[c]:
                copy.wait()
            value_acc[c] = jnp.zeros((slots, HEAD_SIZE), F32)
        attention(c, first, last)

    attend(0, 0, 4)
    pl.semaphore_wait(barrier, dp_count + fsdp_count + tensor_count - 3)
    send_scalars(0, totals)
    attend(0, 4, QUERY_PER_VALUE)
    totals = add_scalars(0, totals)
    send_scalars(1, totals)
    attend(1)
    totals = add_scalars(1, totals)
    count = F32(blocks)
    value_weight = (own_reward[:1] - totals[0:1] / count) * count / totals[1:2]
    hidden_load.wait()

    pending = {u: 0 for u in range(2 * heads)}

    def advance_head(k, c):
        for u in (2 * c, 2 * c + 1):
            advance(k, u)
            pending[u] = k + 1

    for c in range(heads):
        value_t[...] = (value_acc[c] * value_weight).T.astype(BF16)
        for begin in (sent_at[0], kept_at[0]):
            multiply(c, begin, half_of[0])
            if begin is sent_at[0]:
                reduce_copy(0, 2 * c).start()
                reduce_copy(0, 2 * c + 1).start()
        advance_head(0, c)
        if c + 2 < heads:
            attend(c + 2)
        if 0 < c < heads - 1:
            advance_head(1, c - 1)
        elif c == heads - 1:
            advance_head(2, 0)
    for copy in state_loads:
        copy.wait()
    for step in range(2 * heads + stages - 2):
        for k in reversed(range(1, stages)):
            u = step - (k - 1)
            if 0 <= u < 2 * heads and pending[u] <= k:
                if k < stages - 1:
                    advance(k, u)
                elif u % 2 == 1:
                    finish(u // 2)

    for c in range(heads):
        for d in range(1, tensor_count):
            swap_copy(d, c).wait_recv()
    for c in range(heads):
        wanted = layout_ref[tensor * heads + c]
        back = (tensor - wanted // heads + tensor_count) % tensor_count
        rollout_out[:, c * HEAD_SIZE : (c + 1) * HEAD_SIZE] = heads_all[back * heads + wanted % heads]
    for k in range(stages):
        for u in range(2 * heads):
            reduce_copy(k, u).wait_send()
    for copy in scalar_copies(0) + scalar_copies(1):
        copy.wait_send()
    for c in range(heads):
        for d in range(1, tensor_count):
            swap_copy(d, c).wait_send()


def fused_step(
    sizes, hidden_in, queries, keys, output_gradient, rewards, lengths, master, moment, second, layout
):
    dp_count, fsdp_count, tensor_count = sizes
    blocks = dp_count * fsdp_count
    stages = log2_of(blocks)
    slots = hidden_in.shape[0]
    rows = master.shape[0]
    heads = keys.shape[1] // HEAD_SIZE
    smem = pl.BlockSpec(memory_space=pltpu.SMEM)
    vmem = pl.BlockSpec(memory_space=pltpu.VMEM)
    anywhere = pl.BlockSpec(memory_space=pl.ANY)
    dma = pltpu.SemaphoreType.DMA
    grad, rollout = pl.pallas_call(
        functools.partial(step_kernel, sizes),
        out_shape=[
            jax.ShapeDtypeStruct(master.shape, F32),
            jax.ShapeDtypeStruct(master.shape, BF16),
        ],
        in_specs=[smem] * 3 + [anywhere, anywhere, vmem] + [anywhere] * 4,
        out_specs=[vmem] * 2,
        scratch_shapes=[
            pltpu.VMEM(hidden_in.shape, BF16),
            pltpu.VMEM(queries.shape, BF16),
            pltpu.VMEM(queries.shape, BF16),
            pltpu.VMEM(master.shape, F32),
            pltpu.VMEM(master.shape, F32),
            pltpu.VMEM(master.shape, F32),
            pltpu.VMEM((slots, slots), F32),
            pltpu.VMEM((heads, slots, HEAD_SIZE), F32),
            pltpu.VMEM((HEAD_SIZE, slots), BF16),
            pltpu.VMEM((2 * heads, blocks, HEAD_SIZE // 2, rows), BF16),
            pltpu.VMEM((2 * heads, blocks - 1, HEAD_SIZE // 2, rows), BF16),
            pltpu.VMEM((tensor_count * heads, rows, HEAD_SIZE), BF16),
            pltpu.VMEM((2, 8, 128), F32),
            pltpu.VMEM((dp_count + fsdp_count - 2, 8, 128), F32),
            dma((2 * heads + 4,)),
            dma((stages, 2 * heads)),
            dma((stages, 2 * heads)),
            dma((dp_count + fsdp_count - 2,)),
            dma((dp_count + fsdp_count - 2,)),
            dma((tensor_count - 1, heads)),
            dma((tensor_count - 1, heads)),
        ],
        compiler_params=pltpu.CompilerParams(
            collective_id=0, has_side_effects=True, vmem_limit_bytes=60 * 1024 * 1024
        ),
    )(rewards, lengths, layout, hidden_in, queries, keys, output_gradient, master, moment, second)
    new_moment, new_second, weight = adam(grad, moment, second, master)
    return weight, new_moment, new_second, rollout


def value_grad(query_matrix, key_matrix, out_rows, value_weight, length):
    token_slot_index = query_matrix.shape[0]
    heads_local = key_matrix.shape[1] // HEAD_SIZE
    query_head_rows = query_matrix.reshape(
        token_slot_index, heads_local, QUERY_PER_VALUE, HEAD_SIZE
    )
    key_head_rows = key_matrix.reshape(token_slot_index, heads_local, HEAD_SIZE)
    scores = jnp.einsum(
        "tkgd,skd->kgts", query_head_rows, key_head_rows, preferred_element_type=jnp.float32
    ) / jnp.sqrt(jnp.float32(HEAD_SIZE))
    position = jnp.arange(token_slot_index)
    allowed = (position[None, :] <= position[:, None]) & (position[None, :] < length)
    scores = jnp.where(allowed[None, None], scores, jnp.float32(-1e30))
    top = jnp.max(scores, axis=-1, keepdims=True)
    expo = jnp.exp(scores - top)
    probs = (expo / jnp.sum(expo, axis=-1, keepdims=True)).astype(jnp.bfloat16)
    attention_gradient = (value_weight[:, None] * out_rows.astype(jnp.float32)).astype(jnp.bfloat16)
    head_gradient = attention_gradient.reshape(
        token_slot_index, heads_local, QUERY_PER_VALUE, HEAD_SIZE
    )
    value_gradient = jnp.einsum(
        "kgts,tkgd->skd", probs, head_gradient, preferred_element_type=jnp.float32
    )
    return value_gradient.reshape(token_slot_index, heads_local * HEAD_SIZE).astype(jnp.bfloat16)


def plain_step(
    hidden_in, queries, keys, output_gradient, rewards, lengths, master, moment, second, layout
):
    reward_sum, length_sum = lax.psum(
        (jnp.sum(rewards), jnp.sum(lengths).astype(jnp.float32)), AXES
    )
    seq_count = jnp.float32(lax.axis_size(AXES))
    advantage = rewards[0] - reward_sum / seq_count
    position = jnp.arange(hidden_in.shape[0])
    value_weight = jnp.where(
        position < lengths[0], advantage * seq_count / length_sum, jnp.float32(0.0)
    )
    value_gradient = value_grad(queries, keys, output_gradient, value_weight, lengths[0])
    grad = lax.psum_scatter(
        lax.dot_general(
            hidden_in, value_gradient, (((0,), (0,)), ((), ())), preferred_element_type=jnp.float32
        ),
        AXES,
        scatter_dimension=0,
        tiled=True,
    )
    new_moment, new_second, weight = adam(grad, moment, second, master)
    rounded = weight.astype(jnp.bfloat16)
    row_count = rounded.shape[0]
    heads_local = rounded.shape[1] // HEAD_SIZE
    targets = lax.dynamic_slice_in_dim(layout, lax.axis_index("tensor") * heads_local, heads_local)
    piece = lax.all_gather(rounded, "tensor", axis=1, tiled=True)
    piece_rows = piece.reshape(row_count, piece.shape[1] // HEAD_SIZE, HEAD_SIZE)
    rollout = jnp.take(piece_rows, targets, axis=1).reshape(row_count, heads_local * HEAD_SIZE)
    return weight, new_moment, new_second, rollout


def solution(mesh):
    sizes = tuple(mesh.shape[a] for a in ("dp", "fsdp", "tensor"))

    def on_device(hidden_in, *rest):
        rows = hidden_in.shape[1] // (sizes[0] * sizes[1])
        powers = all(size & (size - 1) == 0 for size in sizes[:2])
        heads = rest[1].shape[1] // HEAD_SIZE
        large = heads > 1 and sizes[0] * sizes[1] >= 16 and min(sizes) > 1
        if rows % 128 == 0 and powers and large:
            return tuple(fused_step(sizes, hidden_in, *rest))
        return plain_step(hidden_in, *rest)

    rows_spec, split_spec = P(AXES, None), P(AXES, "tensor")
    placed = (rows_spec,) + (split_spec,) * 3 + (P(AXES),) * 2 + (split_spec,) * 3 + (P(),)
    return jax.shard_map(
        on_device, mesh=mesh, in_specs=placed, out_specs=(split_spec,) * 4, check_vma=False
    )
```

```python
import functools
import math

import jax
import jax.numpy as jnp
from jax import lax
from jax.experimental import pallas as pl
from jax.experimental.pallas import tpu as pltpu
from jax.sharding import PartitionSpec as P

HEAD_SIZE = 128
QUERY_PER_VALUE = 8
AXES = ("dp", "fsdp")
MESH = pl.DeviceIdType.MESH
F32 = jnp.float32
BF16 = jnp.bfloat16


def log2_of(number):
    return number.bit_length() - 1


def adam(grad, moment, second, master):
    new_moment = 0.9 * moment + 0.1 * grad
    new_second = 0.95 * second + 0.05 * grad * grad
    corrected = new_moment / (1.0 - 0.9**10) / (jnp.sqrt(new_second / (1.0 - 0.95**10)) + 1e-08)
    return new_moment, new_second, master - 0.002 * (corrected + 0.1 * master)


def query_blocks(slots):
    blocks = []
    for start in range(0, slots, 256):
        size = min(256, slots - start)
        blocks.append((start, size, start + size))
    return blocks


def step_kernel(
    sizes,
    rewards_ref,
    lengths_ref,
    layout_ref,
    hidden_hbm,
    queries_hbm,
    keys_ref,
    outgrad_hbm,
    master_hbm,
    moment_hbm,
    second_hbm,
    grad_out,
    rollout_out,
    hidden,
    queries,
    outgrad,
    master_ref,
    moment_ref,
    second_ref,
    bias,
    value_acc,
    value_t,
    part,
    landed,
    heads_all,
    scalar_sent,
    scalar_landed,
    load_sem,
    rs_send,
    rs_recv,
    scalar_send,
    scalar_recv,
    swap_send,
    swap_recv,
):
    dp_count, fsdp_count, tensor_count = sizes
    dp, fsdp, tensor = (lax.axis_index(a) for a in ("dp", "fsdp", "tensor"))
    dp_bits, fsdp_bits = log2_of(dp_count), log2_of(fsdp_count)
    stages = dp_bits + fsdp_bits
    blocks = dp_count * fsdp_count
    slots = hidden_hbm.shape[0]
    rows = master_ref.shape[0]
    heads = keys_ref.shape[1] // HEAD_SIZE
    group = QUERY_PER_VALUE * HEAD_SIZE

    bits, partners = [], []
    for k in range(stages):
        name, index, shift = ("dp", dp, k) if k < dp_bits else ("fsdp", fsdp, k - dp_bits)
        bit = (index // (1 << shift)) % 2
        bits.append(bit)
        partners.append({name: index + (1 - 2 * bit) * (1 << shift)})
    others = [
        [{name: (index + d) % size} for d in range(1, size)]
        for name, index, size in (("dp", dp, dp_count), ("fsdp", fsdp, fsdp_count))
    ]
    peers = [{"tensor": (tensor + d) % tensor_count} for d in range(1, tensor_count)]

    loads = []
    for c in range(heads):
        columns = pl.ds(c * group, group)
        loads.append(
            [
                pltpu.make_async_copy(source.at[:, columns], target.at[:, columns], load_sem.at[2 * c + i])
                for i, (source, target) in enumerate(((queries_hbm, queries), (outgrad_hbm, outgrad)))
            ]
        )
    hidden_load = pltpu.make_async_copy(hidden_hbm, hidden, load_sem.at[2 * heads])
    for copy in loads[0]:
        copy.start()
    hidden_load.start()
    for pair in loads[1:]:
        for copy in pair:
            copy.start()
    state_loads = [
        pltpu.make_async_copy(source, target, load_sem.at[2 * heads + 1 + i])
        for i, (source, target) in enumerate(
            ((master_hbm, master_ref), (moment_hbm, moment_ref), (second_hbm, second_ref))
        )
    ]
    for copy in state_loads:
        copy.start()

    barrier = pltpu.get_barrier_semaphore()
    for target in others[0] + others[1] + peers:
        pl.semaphore_signal(barrier, inc=1, device_id=target, device_id_type=MESH)

    length = lengths_ref[0]
    own_reward = jnp.full((8, 128), rewards_ref[0], F32)
    own_length = jnp.full((8, 128), length, jnp.int32).astype(F32)
    tile_row = lax.broadcasted_iota(jnp.int32, (8, 128), 0)
    totals = jnp.where(tile_row == 0, own_reward, own_length)

    key_pos = lax.broadcasted_iota(jnp.int32, (slots, slots), 0)
    query_pos = lax.broadcasted_iota(jnp.int32, (slots, slots), 1)
    bias[...] = jnp.where((key_pos <= query_pos) & (key_pos < length), 0.0, -1e30).astype(F32)
    exponent = F32(math.log2(math.e) / math.sqrt(HEAD_SIZE))

    def scalar_copies(turn):
        first = turn * (dp_count - 1)
        return [
            pltpu.make_async_remote_copy(
                src_ref=scalar_sent.at[turn],
                dst_ref=scalar_landed.at[first + i],
                send_sem=scalar_send.at[first + i],
                recv_sem=scalar_recv.at[first + i],
                device_id=target,
                device_id_type=MESH,
            )
            for i, target in enumerate(others[turn])
        ]

    def send_scalars(turn, tile):
        scalar_sent[turn] = tile
        for copy in scalar_copies(turn):
            copy.start()

    def add_scalars(turn, tile):
        first = turn * (dp_count - 1)
        for i, copy in enumerate(scalar_copies(turn)):
            copy.wait_recv()
            tile = tile + scalar_landed[first + i]
        return tile

    def query_head(c, j):
        offset = pl.multiple_of((c * QUERY_PER_VALUE + j) * HEAD_SIZE, HEAD_SIZE)
        columns = pl.ds(offset, HEAD_SIZE)
        for start, size, seen in query_blocks(slots):
            scores = lax.dot_general(
                keys_ref[:seen, c * HEAD_SIZE : (c + 1) * HEAD_SIZE],
                queries[start : start + size, columns],
                (((1,), (1,)), ((), ())),
                preferred_element_type=F32,
            )
            scores = scores + bias[:seen, start : start + size]
            top = jnp.max(scores, axis=0, keepdims=True)
            expo = jnp.exp2((scores - top) * exponent)
            total = jnp.sum(expo, axis=0, keepdims=True)
            slot = start + lax.broadcasted_iota(jnp.int32, (1, size), 1)
            inverse = jnp.where(slot < length, 1.0 / total, 0.0)
            probs = (expo * inverse).astype(BF16)
            value_acc[c, :seen, :] += jnp.dot(
                probs, outgrad[start : start + size, columns], preferred_element_type=F32
            )

    def attention(c, first, last):
        @pl.loop(first, last, unroll=True)
        def _(j):
            query_head(c, j)

    def rows_of(position):
        bit = [(position // (1 << (stages - 1 - k))) % 2 for k in range(stages)]
        dp_of = sum(bit[k] * (1 << k) for k in range(dp_bits))
        fsdp_of = sum(bit[dp_bits + k] * (1 << k) for k in range(fsdp_bits))
        return dp_of * fsdp_count + fsdp_of

    sent_at, kept_at, land_at, half_of = [], [], [], []
    base, landing = 0, 0
    for k in range(stages):
        half = blocks >> (k + 1)
        sent_at.append(base + (1 - bits[k]) * half)
        base = base + bits[k] * half
        kept_at.append(base)
        half_of.append(half)
        land_at.append(landing)
        landing += half

    def reduce_copy(k, u):
        return pltpu.make_async_remote_copy(
            src_ref=part.at[u, pl.ds(sent_at[k], half_of[k])],
            dst_ref=landed.at[u, pl.ds(land_at[k], half_of[k])],
            send_sem=rs_send.at[k, u],
            recv_sem=rs_recv.at[k, u],
            device_id=partners[k],
            device_id_type=MESH,
        )

    def multiply(c, begin, count):
        @pl.loop(0, count, unroll=2 if count % 2 == 0 else 1)
        def _(i):
            position = begin + i
            columns = pl.ds(pl.multiple_of(rows_of(position) * rows, 128), rows)
            product = jnp.dot(
                value_t[...], hidden[:, columns], preferred_element_type=F32
            ).astype(BF16)
            part[2 * c, position] = product[: HEAD_SIZE // 2]
            part[2 * c + 1, position] = product[HEAD_SIZE // 2 :]

    def fold(k, u, begin, count):
        @pl.loop(0, count, unroll=2 if count % 2 == 0 else 1)
        def _(i):
            position = begin + i
            arrived = landed[u, land_at[k] + position - kept_at[k]]
            part[u, position] = (part[u, position].astype(F32) + arrived.astype(F32)).astype(BF16)

    def advance(k, u):
        reduce_copy(k, u).wait_recv()
        fold(k, u, sent_at[k + 1], half_of[k + 1])
        reduce_copy(k + 1, u).start()
        fold(k, u, kept_at[k + 1], half_of[k + 1])

    def swap_copy(d, c):
        return pltpu.make_async_remote_copy(
            src_ref=heads_all.at[c],
            dst_ref=heads_all.at[d * heads + c],
            send_sem=swap_send.at[d - 1, c],
            recv_sem=swap_recv.at[d - 1, c],
            device_id=peers[d - 1],
            device_id_type=MESH,
        )

    def arrive(u):
        k = stages - 1
        reduce_copy(k, u).wait_recv()
        return part[u, kept_at[k]].astype(F32) + landed[u, land_at[k]].astype(F32)

    def finish(c):
        total = jnp.concatenate([arrive(2 * c), arrive(2 * c + 1)], axis=0).T
        columns = slice(c * HEAD_SIZE, (c + 1) * HEAD_SIZE)
        _, _, weight = adam(
            total, moment_ref[:, columns], second_ref[:, columns], master_ref[:, columns]
        )
        heads_all[c] = weight.astype(BF16)
        for d in range(1, tensor_count):
            swap_copy(d, c).start()
        grad_out[:, columns] = total

    def attend(c, first=0, last=QUERY_PER_VALUE):
        if first == 0:
            for copy in loads[c]:
                copy.wait()
            value_acc[c] = jnp.zeros((slots, HEAD_SIZE), F32)
        attention(c, first, last)

    attend(0, 0, 4)
    pl.semaphore_wait(barrier, dp_count + fsdp_count + tensor_count - 3)
    send_scalars(0, totals)
    attend(0, 4, QUERY_PER_VALUE)
    totals = add_scalars(0, totals)
    send_scalars(1, totals)
    attend(1)
    totals = add_scalars(1, totals)
    count = F32(blocks)
    value_weight = (own_reward[:1] - totals[0:1] / count) * count / totals[1:2]
    hidden_load.wait()

    pending = {u: 0 for u in range(2 * heads)}

    def advance_head(k, c):
        for u in (2 * c, 2 * c + 1):
            advance(k, u)
            pending[u] = k + 1

    for c in range(heads):
        value_t[...] = (value_acc[c] * value_weight).T.astype(BF16)
        for begin in (sent_at[0], kept_at[0]):
            multiply(c, begin, half_of[0])
            if begin is sent_at[0]:
                reduce_copy(0, 2 * c).start()
                reduce_copy(0, 2 * c + 1).start()
        advance_head(0, c)
        if c + 2 < heads:
            attend(c + 2)
        if 0 < c < heads - 1:
            advance_head(1, c - 1)
        elif c == heads - 1:
            advance_head(2, 0)
    for copy in state_loads:
        copy.wait()
    for step in range(2 * heads + stages - 2):
        for k in reversed(range(1, stages)):
            u = step - (k - 1)
            if 0 <= u < 2 * heads and pending[u] <= k:
                if k < stages - 1:
                    advance(k, u)
                elif u % 2 == 1:
                    finish(u // 2)

    for c in range(heads):
        for d in range(1, tensor_count):
            swap_copy(d, c).wait_recv()
    for c in range(heads):
        wanted = layout_ref[tensor * heads + c]
        back = (tensor - wanted // heads + tensor_count) % tensor_count
        rollout_out[:, c * HEAD_SIZE : (c + 1) * HEAD_SIZE] = heads_all[back * heads + wanted % heads]
    for k in range(stages):
        for u in range(2 * heads):
            reduce_copy(k, u).wait_send()
    for copy in scalar_copies(0) + scalar_copies(1):
        copy.wait_send()
    for c in range(heads):
        for d in range(1, tensor_count):
            swap_copy(d, c).wait_send()


def fused_step(
    sizes, hidden_in, queries, keys, output_gradient, rewards, lengths, master, moment, second, layout
):
    dp_count, fsdp_count, tensor_count = sizes
    blocks = dp_count * fsdp_count
    stages = log2_of(blocks)
    slots = hidden_in.shape[0]
    rows = master.shape[0]
    heads = keys.shape[1] // HEAD_SIZE
    smem = pl.BlockSpec(memory_space=pltpu.SMEM)
    vmem = pl.BlockSpec(memory_space=pltpu.VMEM)
    anywhere = pl.BlockSpec(memory_space=pl.ANY)
    dma = pltpu.SemaphoreType.DMA
    grad, rollout = pl.pallas_call(
        functools.partial(step_kernel, sizes),
        out_shape=[
            jax.ShapeDtypeStruct(master.shape, F32),
            jax.ShapeDtypeStruct(master.shape, BF16),
        ],
        in_specs=[smem] * 3 + [anywhere, anywhere, vmem] + [anywhere] * 4,
        out_specs=[vmem] * 2,
        scratch_shapes=[
            pltpu.VMEM(hidden_in.shape, BF16),
            pltpu.VMEM(queries.shape, BF16),
            pltpu.VMEM(queries.shape, BF16),
            pltpu.VMEM(master.shape, F32),
            pltpu.VMEM(master.shape, F32),
            pltpu.VMEM(master.shape, F32),
            pltpu.VMEM((slots, slots), F32),
            pltpu.VMEM((heads, slots, HEAD_SIZE), F32),
            pltpu.VMEM((HEAD_SIZE, slots), BF16),
            pltpu.VMEM((2 * heads, blocks, HEAD_SIZE // 2, rows), BF16),
            pltpu.VMEM((2 * heads, blocks - 1, HEAD_SIZE // 2, rows), BF16),
            pltpu.VMEM((tensor_count * heads, rows, HEAD_SIZE), BF16),
            pltpu.VMEM((2, 8, 128), F32),
            pltpu.VMEM((dp_count + fsdp_count - 2, 8, 128), F32),
            dma((2 * heads + 4,)),
            dma((stages, 2 * heads)),
            dma((stages, 2 * heads)),
            dma((dp_count + fsdp_count - 2,)),
            dma((dp_count + fsdp_count - 2,)),
            dma((tensor_count - 1, heads)),
            dma((tensor_count - 1, heads)),
        ],
        compiler_params=pltpu.CompilerParams(
            collective_id=0, has_side_effects=True, vmem_limit_bytes=60 * 1024 * 1024
        ),
    )(rewards, lengths, layout, hidden_in, queries, keys, output_gradient, master, moment, second)
    new_moment, new_second, weight = adam(grad, moment, second, master)
    return weight, new_moment, new_second, rollout


def value_grad(query_matrix, key_matrix, out_rows, value_weight, length):
    token_slot_index = query_matrix.shape[0]
    heads_local = key_matrix.shape[1] // HEAD_SIZE
    query_head_rows = query_matrix.reshape(
        token_slot_index, heads_local, QUERY_PER_VALUE, HEAD_SIZE
    )
    key_head_rows = key_matrix.reshape(token_slot_index, heads_local, HEAD_SIZE)
    scores = jnp.einsum(
        "tkgd,skd->kgts", query_head_rows, key_head_rows, preferred_element_type=jnp.float32
    ) / jnp.sqrt(jnp.float32(HEAD_SIZE))
    position = jnp.arange(token_slot_index)
    allowed = (position[None, :] <= position[:, None]) & (position[None, :] < length)
    scores = jnp.where(allowed[None, None], scores, jnp.float32(-1e30))
    top = jnp.max(scores, axis=-1, keepdims=True)
    expo = jnp.exp(scores - top)
    probs = (expo / jnp.sum(expo, axis=-1, keepdims=True)).astype(jnp.bfloat16)
    attention_gradient = (value_weight[:, None] * out_rows.astype(jnp.float32)).astype(jnp.bfloat16)
    head_gradient = attention_gradient.reshape(
        token_slot_index, heads_local, QUERY_PER_VALUE, HEAD_SIZE
    )
    value_gradient = jnp.einsum(
        "kgts,tkgd->skd", probs, head_gradient, preferred_element_type=jnp.float32
    )
    return value_gradient.reshape(token_slot_index, heads_local * HEAD_SIZE).astype(jnp.bfloat16)


def plain_step(
    hidden_in, queries, keys, output_gradient, rewards, lengths, master, moment, second, layout
):
    reward_sum, length_sum = lax.psum(
        (jnp.sum(rewards), jnp.sum(lengths).astype(jnp.float32)), AXES
    )
    seq_count = jnp.float32(lax.axis_size(AXES))
    advantage = rewards[0] - reward_sum / seq_count
    position = jnp.arange(hidden_in.shape[0])
    value_weight = jnp.where(
        position < lengths[0], advantage * seq_count / length_sum, jnp.float32(0.0)
    )
    value_gradient = value_grad(queries, keys, output_gradient, value_weight, lengths[0])
    grad = lax.psum_scatter(
        lax.dot_general(
            hidden_in, value_gradient, (((0,), (0,)), ((), ())), preferred_element_type=jnp.float32
        ),
        AXES,
        scatter_dimension=0,
        tiled=True,
    )
    new_moment, new_second, weight = adam(grad, moment, second, master)
    rounded = weight.astype(jnp.bfloat16)
    row_count = rounded.shape[0]
    heads_local = rounded.shape[1] // HEAD_SIZE
    targets = lax.dynamic_slice_in_dim(layout, lax.axis_index("tensor") * heads_local, heads_local)
    piece = lax.all_gather(rounded, "tensor", axis=1, tiled=True)
    piece_rows = piece.reshape(row_count, piece.shape[1] // HEAD_SIZE, HEAD_SIZE)
    rollout = jnp.take(piece_rows, targets, axis=1).reshape(row_count, heads_local * HEAD_SIZE)
    return weight, new_moment, new_second, rollout


def solution(mesh):
    sizes = tuple(mesh.shape[a] for a in ("dp", "fsdp", "tensor"))

    def on_device(hidden_in, *rest):
        rows = hidden_in.shape[1] // (sizes[0] * sizes[1])
        powers = all(size & (size - 1) == 0 for size in sizes[:2])
        heads = rest[1].shape[1] // HEAD_SIZE
        large = heads > 1 and sizes[0] * sizes[1] >= 16 and min(sizes) > 1
        if rows % 128 == 0 and powers and large:
            return tuple(fused_step(sizes, hidden_in, *rest))
        return plain_step(hidden_in, *rest)

    rows_spec, split_spec = P(AXES, None), P(AXES, "tensor")
    placed = (rows_spec,) + (split_spec,) * 3 + (P(AXES),) * 2 + (split_spec,) * 3 + (P(),)
    return jax.shard_map(
        on_device, mesh=mesh, in_specs=placed, out_specs=(split_spec,) * 4, check_vma=False
    )
```
